32 devices in a mesh: tok: 8 (over z, x), head: 4 (over y, core).
Axes of the slice: x: 2, y: 2, z: 4, core: 2. Of those that a mesh axis runs over, the one named last changes fastest.
Arguments:
- queries: bfloat16 [1024, 2048], P('tok', 'head'), may hold values from -32 to 32, as said below
- key_rows: bfloat16 [1024, 2048], P('tok', 'head'), may hold values from -16 to 16
- value_rows: bfloat16 [1024, 2048], P('tok', 'head'), may hold values from -6 to 6
- learn_rates: float32 [1024, 4], P('tok', 'head'), may hold values from 0.25 to 12, as said below
- fast_weights: bfloat16 [4, 3, 512, 512], P('head'), may hold values from -0.25 to 0.25
- out_weight: bfloat16 [2048, 2048], P(None, 'head'), may hold values from -0.5 to 0.5
Outputs:
- layer_out: bfloat16 [1024, 2048], P('tok', 'head')
The draws below stay inside these ranges and needn't reach their ends.
Inputs may be any that keep to these rules, and one draw needn't show every extreme that they name: `queries`: queries drawn together with the keys. `learn_rates`: Positive.
All inputs are finite; a program needn't handle non-finite values.
Results may differ from the reference program's by a relative error of at most 0.019.
Values may be sent and summed in bfloat16 or wider, within the bound.
A program may use at most 64 MiB of HBM per device.

```python
import math
import jax
import jax.numpy as jnp
from jax import lax

H = 4
HD = 512
TOK_DEV = 128
WIN = 1024
NS_STEPS = 2
D = 2048
TOKENS = 1024


def joint_fields(key):
    base = jax.random.fold_in(key, 4242)
    key_draw, query_draw = jax.random.split(base, 2)
    field_shape = (TOKENS, H, HD)
    key_vals = jax.random.truncated_normal(key_draw, -6.0, 6.0, field_shape, jnp.float32)
    query_vals = jax.random.truncated_normal(query_draw, -6.0, 6.0, field_shape, jnp.float32)
    return (query_vals.reshape(TOKENS, H * HD), key_vals.reshape(TOKENS, H * HD))


def draw_queries(key, part):
    return joint_fields(key)[0].astype(jnp.bfloat16)


def draw_key_rows(key, part):
    return joint_fields(key)[1].astype(jnp.bfloat16)


def draw_learn_rates(key, part):
    noise_key = jax.random.fold_in(key, 99)
    ramp = 1.0 + 2.0 * jnp.arange(TOKENS, dtype=jnp.float32)[:, None] / TOKENS
    base = jnp.exp(jax.random.uniform(noise_key, (TOKENS, H), jnp.float32, math.log(0.25), math.log(4.0)))
    return base * ramp


def block_scale(key, dims, cuts, smallest, largest):
    def one(axis_at, shards_of):
        draws = jax.random.uniform(jax.random.fold_in(jax.random.fold_in(key, 6), axis_at), (shards_of,), jnp.float32, smallest / len(cuts), largest / len(cuts))
        return jnp.repeat(jnp.exp(draws), dims[axis_at] // shards_of).reshape((-1,) + (1,) * (len(dims) - axis_at - 1))

    gain = one(*cuts[0])
    for cut in cuts[1:]:
        gain = gain * one(*cut)
    return gain


def centred(own_key, dims, width, most, pieces=(), kind=jnp.bfloat16):
    array = width * jax.random.normal(own_key, dims, jnp.float32)
    if pieces:
        array = array * block_scale(own_key, dims, pieces, -0.22, 0.18)
    return jnp.clip(array, -most, most).astype(kind)


def setup_inputs(seed: int = 0) -> dict:
    splits = jax.random.split(jax.random.key(seed), 7)
    queries = draw_queries(jax.random.fold_in(splits[6], 71), 0)
    key_rows = draw_key_rows(jax.random.fold_in(splits[6], 71), 0)
    value_rows = centred(splits[2], (TOKENS, D), 1.0, 6.0, ((0, 8), (1, 4)))
    learn_rates = draw_learn_rates(jax.random.fold_in(splits[6], 71), 0)
    fast_weights = centred(splits[4], (H, 3, HD, HD), HD ** -0.5, 0.25, ((0, 4),))
    out_weight = centred(splits[5], (D, D), (D // 16) ** -0.5, 0.5, ((1, 4),))
    return dict(queries=queries, key_rows=key_rows, value_rows=value_rows, learn_rates=learn_rates, fast_weights=fast_weights, out_weight=out_weight)


ns_first = 3.4445
ns_second = -4.775
ns_third = 2.0315
update_rate = 2.0
fw_scale = 0.5
eps = 1e-06

def rms_norm(values):
    values = values.astype(jnp.float32)
    return values * lax.rsqrt(lax.optimization_barrier(jnp.mean(values * values, axis=-1, keepdims=True)) + eps)

def contract_first(left, right):
    return lax.dot_general(left, right, (((0,), (0,)), ((), ())), preferred_element_type=jnp.float32)

def contract_last(left, right):
    return lax.dot_general(left, right, (((1,), (1,)), ((), ())), preferred_element_type=jnp.float32)

def block_attend(query_block, key_block, value_block, offset):
    scores = contract_last(query_block, key_block) * HD ** (-0.5)
    row_ids = lax.broadcasted_iota(jnp.int32, scores.shape, 0)
    col_ids = lax.broadcasted_iota(jnp.int32, scores.shape, 1)
    allowed = (col_ids > row_ids) & (col_ids <= row_ids + WIN) & (col_ids >= WIN - offset)
    scores = jnp.where(allowed, scores, -jnp.inf)
    top_score = lax.optimization_barrier(jnp.max(scores, axis=1, keepdims=True))
    weights = jnp.exp(scores - top_score)
    totals = lax.optimization_barrier(jnp.sum(weights, axis=1, keepdims=True))
    probs = (weights / totals).astype(jnp.bfloat16)
    return jnp.dot(probs, value_block, preferred_element_type=jnp.float32)

def window_attention(query_all, key_all, value_all):
    padding = jnp.zeros((WIN, HD), key_all.dtype)
    key_padded = jnp.concatenate([padding, key_all], axis=0)
    value_padded = jnp.concatenate([padding, value_all], axis=0)

    def one_block(block_index):
        offset = (block_index * TOK_DEV).astype(jnp.int32)
        query_block = lax.dynamic_slice_in_dim(query_all, offset, TOK_DEV, 0)
        key_block = lax.dynamic_slice_in_dim(key_padded, offset, WIN + TOK_DEV, 0)
        value_block = lax.dynamic_slice_in_dim(value_padded, offset, WIN + TOK_DEV, 0)
        return block_attend(query_block, key_block, value_block, offset)
    blocks = lax.map(one_block, jnp.arange(TOKENS // TOK_DEV, dtype=jnp.int32))
    return blocks.reshape(TOKENS, HD)

def fast_grads(key_part, value_part, rate_part, weights):
    key_norm = rms_norm(key_part).astype(jnp.bfloat16)
    gate = jnp.dot(key_norm, weights[0], preferred_element_type=jnp.float32)
    up_part = jnp.dot(key_norm, weights[1], preferred_element_type=jnp.float32)
    sigmoid_gate = jax.nn.sigmoid(gate)
    activated = gate * sigmoid_gate
    hidden = (activated * up_part).astype(jnp.bfloat16)
    scaled = (rate_part[:, None] * value_part.astype(jnp.float32)).astype(jnp.bfloat16)
    back = contract_last(scaled, weights[2])
    d_gate = (back * up_part * sigmoid_gate * (1.0 + gate * (1.0 - sigmoid_gate))).astype(jnp.bfloat16)
    d_up = (back * activated).astype(jnp.bfloat16)
    return jnp.stack([contract_first(key_norm, d_gate), contract_first(key_norm, d_up), contract_first(hidden, scaled)])

def orthogonalize(grads):
    norms = jnp.sqrt(lax.optimization_barrier(jnp.sum(grads * grads, axis=(1, 2), keepdims=True)))
    iterate = (grads / (norms + eps)).astype(jnp.bfloat16)
    for sweep in range(NS_STEPS):
        wide = iterate.astype(jnp.float32)
        gram = jnp.einsum('mij,mkj->mik', wide, wide, precision=lax.Precision.HIGHEST).astype(jnp.bfloat16)
        cross = jnp.einsum('mik,mkj->mij', gram.astype(jnp.float32), wide, precision=lax.Precision.HIGHEST).astype(jnp.bfloat16)
        square = jnp.einsum('mik,mkj->mij', gram.astype(jnp.float32), cross.astype(jnp.float32), precision=lax.Precision.HIGHEST)
        iterate = (ns_first * wide + ns_second * cross.astype(jnp.float32) + ns_third * square).astype(jnp.bfloat16)
    return iterate

def fast_apply(query_part, weights):
    query_norm = rms_norm(query_part).astype(jnp.bfloat16)
    gate = jnp.dot(query_norm, weights[0], preferred_element_type=jnp.float32)
    up_part = jnp.dot(query_norm, weights[1], preferred_element_type=jnp.float32)
    q_hidden = (jax.nn.silu(gate) * up_part).astype(jnp.bfloat16)
    return jnp.dot(q_hidden, weights[2], preferred_element_type=jnp.float32)

def reference(queries, key_rows, value_rows, learn_rates, fast_weights, out_weight):
    mixed_heads = []
    for head_index in range(H):
        lower = head_index * HD
        query_part = queries[:, lower:lower + HD]
        key_part = key_rows[:, lower:lower + HD]
        value_part = value_rows[:, lower:lower + HD]
        attended = window_attention(query_part, key_part, value_part)
        grads = fast_grads(key_part, value_part, learn_rates[:, head_index], fast_weights[head_index])
        ortho = orthogonalize(grads)
        updated = (fast_weights[head_index].astype(jnp.float32) + update_rate * ortho.astype(jnp.float32)).astype(jnp.bfloat16)
        applied = fast_apply(query_part, updated)
        mixed_heads.append((attended + fw_scale * rms_norm(applied)).astype(jnp.bfloat16))
    mixed = jnp.concatenate(mixed_heads, axis=1)
    return jnp.dot(mixed, out_weight, preferred_element_type=jnp.float32).astype(jnp.bfloat16)
```

```python
import functools

import jax
import jax.numpy as jnp
from jax import lax
from jax.experimental import pallas as pl
from jax.experimental.pallas import tpu as pltpu
from jax.sharding import PartitionSpec as P

HD = 512
WIN = 1024
NS_STEPS = 2
PAIR = 2


ns_first = 3.4445
ns_second = -4.775
ns_third = 2.0315
update_rate = 2.0
fw_scale = 0.5
eps = 1e-06

MESH = pl.DeviceIdType.MESH


def passed_along(block, axis, distance):
    devices = range(lax.axis_size(axis))
    route = [(i - distance, i) for i in devices if i - distance in devices]
    return lax.ppermute(block, axis, route)


def rms_norm(values):
    values = values.astype(jnp.float32)
    return values * lax.rsqrt(jnp.mean(values * values, axis=-1, keepdims=True) + eps)


def contract_first(left, right):
    return lax.dot_general(
        left, right, (((0,), (0,)), ((), ())), preferred_element_type=jnp.float32
    )


def contract_last(left, right):
    return lax.dot_general(
        left, right, (((1,), (1,)), ((), ())), preferred_element_type=jnp.float32
    )


def matmul(left, right):
    return jnp.dot(left, right, preferred_element_type=jnp.float32)


def block_orders(depth):
    orders = []
    for z in range(depth):
        waiting = []
        for zp in range(depth):
            apart = abs(z - zp)
            waiting.append((2 * apart, zp * 2 + 1, max(0, 2 * apart - 1)))
            waiting.append((2 * apart + 2, zp * 2, 2 * apart + 1))
        order = []
        for t in range(2 * depth):
            ready = [entry for entry in waiting if entry[2] <= t]
            best = min(ready, key=lambda entry: (entry[0], -(entry[1] % 2), entry[1]))
            waiting.remove(best)
            order.append(best[1])
        orders.append(order)
    return orders


def fused_kernel(
    n_tok,
    q_hbm, k_hbm, v_hbm, rate_hbm, weights_hbm, out_hbm, result,
    q_ref, k_buf, v_buf, r_ref, w_ref, ow_ref,
    grads, ortho, gram_ref, cross_ref,
    top_ref, total_ref, acc_ref, heads_buf,
    local_sem, recv_sem, up_sem, down_sem, pair_sem,
    head_recv, head_send,
):
    rows, width = q_ref.shape
    depth = n_tok // PAIR
    me = lax.axis_index("tok")
    head = lax.axis_index("head")
    z = me // PAIR
    x = me % PAIR
    other = (PAIR - 1) - x
    core_peer = head + 1 - 2 * (head % 2)
    row_peer = (head + 2) % 4
    bufs = (k_buf, v_buf)
    panels = width // rows
    tail = panels * rows

    def local_copy(source, target, index):
        return pltpu.make_async_copy(source, target, local_sem.at[index])

    loads = [
        local_copy(k_hbm, k_buf.at[me], 0),
        local_copy(rate_hbm, r_ref, 1),
        local_copy(out_hbm, ow_ref, 2),
        local_copy(weights_hbm.at[0], w_ref, 3),
        local_copy(q_hbm, q_ref, 4),
    ]
    value_loads = [
        local_copy(
            v_hbm.at[:, pl.ds(panel * rows, rows)],
            v_buf.at[me, pl.ds(panel * rows, rows)],
            5 + panel,
        )
        for panel in range(panels)
    ]
    for load in value_loads + loads[:2] + loads[3:] + loads[2:3]:
        load.start()

    barrier = pltpu.get_barrier_semaphore()

    @pl.when(z > 0)
    def _():
        pl.semaphore_signal(barrier, inc=1, device_id={"tok": me - PAIR}, device_id_type=MESH)

    @pl.when(z < depth - 1)
    def _():
        pl.semaphore_signal(barrier, inc=1, device_id={"tok": me + PAIR}, device_id_type=MESH)

    pl.semaphore_signal(
        barrier, inc=1, device_id={"tok": z * PAIR + other}, device_id_type=MESH
    )
    pl.semaphore_signal(barrier, inc=1, device_id={"head": core_peer}, device_id_type=MESH)
    pl.semaphore_signal(barrier, inc=1, device_id={"head": row_peer}, device_id_type=MESH)
    has_lower = jnp.where(z > 0, 1, 0)
    has_upper = jnp.where(z < depth - 1, 1, 0)
    pl.semaphore_wait(barrier, 3 + has_lower + has_upper)

    def hop(slot, piece, sems, target, own=False):
        source = k_hbm if own else bufs[piece].at[slot]
        return pltpu.make_async_remote_copy(
            src_ref=source,
            dst_ref=bufs[piece].at[slot],
            send_sem=sems.at[slot, piece],
            recv_sem=recv_sem.at[slot, piece],
            device_id={"tok": target},
            device_id_type=MESH,
        )

    def each_hop(zp, piece, action, own=False):
        slot = zp * PAIR + x

        @pl.when((zp <= z) & (z < depth - 1))
        def _():
            action(hop(slot, piece, up_sem, me + PAIR, own))

        @pl.when((zp >= z) & (z > 0))
        def _():
            action(hop(slot, piece, down_sem, me - PAIR, own))

        def across():
            action(hop(slot, piece, pair_sem, z * PAIR + other, own))

        if piece == 1:
            pl.when((zp == z) | ((zp > 0) & (zp < depth - 1)))(across)
        else:
            across()

    def each_detour(zp, action):
        slot = zp * PAIR + other

        @pl.when((zp == 0) & (z < depth - 1))
        def _():
            action(hop(slot, 1, up_sem, me + PAIR))

        @pl.when((zp == depth - 1) & (z > 0))
        def _():
            action(hop(slot, 1, down_sem, me - PAIR))

    def start(copy):
        copy.start()

    def arrive(slot, piece):
        hop(slot, piece, pair_sem, z * PAIR + other).wait_recv()

    each_hop(z, 0, start, own=True)
    for load in value_loads:
        load.wait()
    loads[1].wait()
    rest = r_ref[...]
    digits = []
    for _ in range(3):
        digit = rest.astype(jnp.bfloat16)
        rest = rest - digit.astype(jnp.float32)
        digits.append(digit.astype(jnp.float32))
    digits.append(jnp.zeros((13, rows), jnp.float32))
    v_buf[me, tail:, :] = jnp.concatenate(digits, axis=0).astype(jnp.bfloat16)
    each_hop(z, 1, start)

    def value(slot):
        return jnp.concatenate(
            [v_buf[slot, panel * rows : (panel + 1) * rows, :] for panel in range(panels)],
            axis=1,
        )

    orders = block_orders(depth)

    def at_place(values, place):
        chosen = values[0]
        for index in range(1, len(values)):
            chosen = jnp.where(place == index, values[index], chosen)
        return chosen

    mine = [at_place([order[t] for order in orders], z) for t in range(n_tok)]

    grads[...] = jnp.zeros_like(grads)
    top_ref[...] = jnp.full_like(top_ref, -1e30)
    total_ref[...] = jnp.zeros_like(total_ref)
    acc_ref[...] = jnp.zeros_like(acc_ref)
    loads[0].wait()
    for load in loads[3:]:
        load.wait()

    def attend(slot):
        scores = contract_last(q_ref[...], k_buf[slot]) * HD ** (-0.5)
        row_ids = lax.broadcasted_iota(jnp.int32, scores.shape, 0) + me * rows
        col_ids = lax.broadcasted_iota(jnp.int32, scores.shape, 1) + slot * rows
        scores = jnp.where(col_ids <= row_ids, scores, -1e30)
        top = top_ref[:, :1]
        new_top = jnp.maximum(top, jnp.max(scores, axis=1, keepdims=True))
        fade = jnp.exp(top - new_top)
        shares = jnp.exp(scores - new_top)
        total = total_ref[:, :1] * fade + jnp.sum(shares, axis=1, keepdims=True)
        acc_ref[...] = acc_ref[...] * fade + matmul(shares.astype(jnp.bfloat16), value(slot))
        top_ref[...] = jnp.broadcast_to(new_top, top_ref.shape)
        total_ref[...] = jnp.broadcast_to(total, total_ref.shape)

    def learn(slot):
        key_norm = rms_norm(k_buf[slot]).astype(jnp.bfloat16)
        digits = v_buf[slot, tail:, :].astype(jnp.float32)
        rates = (digits[0:1] + digits[1:2]) + digits[2:3]
        rates = jnp.broadcast_to(rates, (rows, rows)).T[:, :1]
        scaled = (rates * value(slot).astype(jnp.float32)).astype(jnp.bfloat16)
        gate = matmul(key_norm, w_ref[0])
        up_part = matmul(key_norm, w_ref[1])
        back = contract_last(scaled, w_ref[2])
        sigmoid_gate = jax.nn.sigmoid(gate)
        activated = gate * sigmoid_gate
        hidden = (activated * up_part).astype(jnp.bfloat16)
        d_gate = (back * up_part * sigmoid_gate * (1.0 + gate * (1.0 - sigmoid_gate))).astype(
            jnp.bfloat16
        )
        d_up = (back * activated).astype(jnp.bfloat16)
        grads[0] += contract_first(key_norm, d_gate)
        grads[1] += contract_first(key_norm, d_up)
        grads[2] += contract_first(hidden, scaled)

    def both_ways(distance, action):
        @pl.when(z - distance >= 0)
        def _():
            action(z - distance)

        @pl.when(z + distance < depth)
        def _():
            action(z + distance)

    def pass_on(*pieces):
        def action(zp):
            for piece in pieces:
                arrive(zp * PAIR + x, piece)
                each_hop(zp, piece, start)

        return action

    def turned(zp):
        return ((zp == 0) & (z < depth - 1)) | ((zp == depth - 1) & (z > 0))

    def pass_detour(zp):
        @pl.when(turned(zp))
        def _():
            arrive(zp * PAIR + other, 1)

        each_detour(zp, start)

    def step(t, carry):
        code = at_place(mine, t)
        own_column = code % 2 == 1
        zp = code // 2
        slot = zp * PAIR + jnp.where(own_column, x, other)

        @pl.when(t == 1)
        def _():
            both_ways(1, pass_on(0))
            pass_detour(z)

        @pl.when((t % 2 == 1) & (t > 1))
        def _():
            both_ways((t - 1) // 2, pass_detour)

        @pl.when(t % 2 == 1)
        def _():
            both_ways((t + 1) // 2, pass_on(1))

        @pl.when((t % 2 == 0) & (t > 0))
        def _():
            both_ways(t // 2 + 1, pass_on(0))

        @pl.when(jnp.logical_not(own_column))
        def _():
            arrive(slot, 0)

            @pl.when(jnp.logical_not(turned(zp)))
            def _():
                arrive(slot, 1)

        @pl.when(slot <= me)
        def _():
            attend(slot)

        learn(slot)
        return carry

    lax.fori_loop(0, n_tok, step, 0)

    for m in range(3):
        summed = grads[m]
        norm = jnp.sqrt(jnp.sum(jnp.sum(summed * summed, axis=0, keepdims=True), axis=1, keepdims=True))
        ortho[m] = (summed / (norm + eps)).astype(jnp.bfloat16)

    def sweep(index, carry):
        for m in range(3):
            gram_ref[m] = contract_last(ortho[m], ortho[m]).astype(jnp.bfloat16)
        for m in range(3):
            cross_ref[m] = matmul(gram_ref[m], ortho[m]).astype(jnp.bfloat16)
        for m in range(3):
            square = matmul(gram_ref[m], cross_ref[m])
            ortho[m] = (
                ns_first * ortho[m].astype(jnp.float32)
                + ns_second * cross_ref[m].astype(jnp.float32)
                + ns_third * square
            ).astype(jnp.bfloat16)
        return carry

    lax.fori_loop(0, NS_STEPS, sweep, 0)

    def updated(m):
        return (
            w_ref[m].astype(jnp.float32) + update_rate * ortho[m].astype(jnp.float32)
        ).astype(jnp.bfloat16)

    query_norm = rms_norm(q_ref[...]).astype(jnp.bfloat16)
    gate = matmul(query_norm, updated(0))
    up_part = matmul(query_norm, updated(1))
    q_hidden = (jax.nn.silu(gate) * up_part).astype(jnp.bfloat16)
    applied = matmul(q_hidden, updated(2))
    attended = acc_ref[...] / total_ref[:, :1]
    heads_buf[head] = (attended + fw_scale * rms_norm(applied)).astype(jnp.bfloat16)

    def head_copy(block, sem, target):
        return pltpu.make_async_remote_copy(
            src_ref=heads_buf.at[block],
            dst_ref=heads_buf.at[block],
            send_sem=head_send.at[sem],
            recv_sem=head_recv.at[block],
            device_id={"head": target},
            device_id_type=MESH,
        )

    to_row = head_copy(head, 0, row_peer)
    to_core = head_copy(head, 1, core_peer)
    relay = head_copy(row_peer, 2, core_peer)
    corner = (core_peer + 2) % 4
    to_row.start()
    to_core.start()
    loads[2].wait()

    def project(block):
        first = pl.multiple_of(block * width, width)
        return matmul(heads_buf[block], ow_ref[pl.ds(first, width), :])

    projected = project(head)
    head_copy(core_peer, 1, core_peer).wait_recv()
    projected += project(core_peer)
    head_copy(row_peer, 0, row_peer).wait_recv()
    relay.start()
    projected += project(row_peer)
    head_copy(corner, 2, core_peer).wait_recv()
    projected += project(corner)
    result[...] = projected.astype(result.dtype)

    to_row.wait_send()
    to_core.wait_send()
    relay.wait_send()

    def finish(copy):
        copy.wait_send()

    def drain(zp, carry):
        for piece in (0, 1):
            each_hop(zp, piece, finish)
        each_detour(zp, finish)
        return carry

    lax.fori_loop(0, depth, drain, 0)


def fused_body(queries, key_rows, value_rows, learn_rates, fast_weights, out_weight):
    rows, width = queries.shape
    n_tok = lax.axis_size("tok")
    n_head = lax.axis_size("head")
    columns = out_weight.shape[1]
    dma = pltpu.SemaphoreType.DMA
    return pl.pallas_call(
        functools.partial(fused_kernel, n_tok),
        out_shape=jax.ShapeDtypeStruct((rows, columns), jnp.bfloat16),
        in_specs=[pl.BlockSpec(memory_space=pl.ANY)] * 6,
        out_specs=pl.BlockSpec(memory_space=pltpu.VMEM),
        scratch_shapes=[
            pltpu.VMEM((rows, width), jnp.bfloat16),
            pltpu.VMEM((n_tok, rows, width), jnp.bfloat16),
            pltpu.VMEM((n_tok, width + 16, rows), jnp.bfloat16),
            pltpu.VMEM((1, rows), jnp.float32),
            pltpu.VMEM(fast_weights.shape[1:], jnp.bfloat16),
            pltpu.VMEM(out_weight.shape, jnp.bfloat16),
            pltpu.VMEM(fast_weights.shape[1:], jnp.float32),
            pltpu.VMEM(fast_weights.shape[1:], jnp.bfloat16),
            pltpu.VMEM(fast_weights.shape[1:], jnp.bfloat16),
            pltpu.VMEM(fast_weights.shape[1:], jnp.bfloat16),
            pltpu.VMEM((rows, 128), jnp.float32),
            pltpu.VMEM((rows, 128), jnp.float32),
            pltpu.VMEM((rows, width), jnp.float32),
            pltpu.VMEM((n_head, rows, width), jnp.bfloat16),
            dma((5 + width // rows,)),
            dma((n_tok, 2)),
            dma((n_tok, 2)),
            dma((n_tok, 2)),
            dma((n_tok, 2)),
            dma((n_head,)),
            dma((3,)),
        ],
        compiler_params=pltpu.CompilerParams(
            collective_id=0, has_side_effects=True, vmem_limit_bytes=48*1024*1024
        ),
    )(*[pltpu.with_memory_space_constraint(a, pltpu.HBM) for a in (queries, key_rows, value_rows, learn_rates.reshape(1, rows), fast_weights, out_weight)])


def block_attend(query_block, key_block, value_block, offset):
    scores = contract_last(query_block, key_block) * HD ** (-0.5)
    row_ids = lax.broadcasted_iota(jnp.int32, scores.shape, 0)
    col_ids = lax.broadcasted_iota(jnp.int32, scores.shape, 1)
    allowed = (col_ids > row_ids) & (col_ids <= row_ids + WIN) & (col_ids >= WIN - offset)
    scores = jnp.where(allowed, scores, -jnp.inf)
    top_score = jnp.max(scores, axis=1, keepdims=True)
    weights = jnp.exp(scores - top_score)
    totals = jnp.sum(weights, axis=1, keepdims=True)
    probs = (weights / totals).astype(jnp.bfloat16)
    return jnp.dot(probs, value_block, preferred_element_type=jnp.float32)


def fast_grads(key_part, value_part, rate_part, weights):
    key_norm = rms_norm(key_part).astype(jnp.bfloat16)
    gate = jnp.dot(key_norm, weights[0], preferred_element_type=jnp.float32)
    up_part = jnp.dot(key_norm, weights[1], preferred_element_type=jnp.float32)
    sigmoid_gate = jax.nn.sigmoid(gate)
    activated = gate * sigmoid_gate
    hidden = (activated * up_part).astype(jnp.bfloat16)
    scaled = (rate_part[:, None] * value_part.astype(jnp.float32)).astype(jnp.bfloat16)
    back = contract_last(scaled, weights[2])
    d_gate = (back * up_part * sigmoid_gate * (1.0 + gate * (1.0 - sigmoid_gate))).astype(
        jnp.bfloat16
    )
    d_up = (back * activated).astype(jnp.bfloat16)
    return jnp.stack(
        [
            contract_first(key_norm, d_gate),
            contract_first(key_norm, d_up),
            contract_first(hidden, scaled),
        ]
    )


def fast_apply(query_part, weights):
    query_norm = rms_norm(query_part).astype(jnp.bfloat16)
    gate = jnp.dot(query_norm, weights[0], preferred_element_type=jnp.float32)
    up_part = jnp.dot(query_norm, weights[1], preferred_element_type=jnp.float32)
    q_hidden = (jax.nn.silu(gate) * up_part).astype(jnp.bfloat16)
    return jnp.dot(q_hidden, weights[2], preferred_element_type=jnp.float32)


def body(queries, key_rows, value_rows, learn_rates, fast_weights, out_weight):
    tok_rows = queries.shape[0]
    reach_shards = WIN // tok_rows
    offset = lax.axis_index("tok") * tok_rows
    stacked = jnp.stack([key_rows, value_rows])
    earlier = []
    moving = stacked
    for distance in range(reach_shards):
        moving = passed_along(moving, "tok", 1)
        earlier.insert(0, moving)
    window_pairs = jnp.concatenate(earlier + [stacked], axis=1)
    weights = fast_weights[0]
    local_grads = fast_grads(key_rows, value_rows, learn_rates[:, 0], weights)
    attended = block_attend(queries, window_pairs[0], window_pairs[1], offset)
    summed = lax.psum(local_grads, "tok")
    norms = jnp.sqrt(jnp.sum(summed * summed, axis=(1, 2), keepdims=True))
    iterate = (summed / (norms + eps)).astype(jnp.bfloat16)
    for sweep in range(NS_STEPS):
        gram = jnp.einsum(
            "mij,mkj->mik", iterate, iterate, preferred_element_type=jnp.float32
        ).astype(jnp.bfloat16)
        cross = jnp.einsum(
            "mik,mkj->mij", gram, iterate, preferred_element_type=jnp.float32
        ).astype(jnp.bfloat16)
        square = jnp.einsum("mik,mkj->mij", gram, cross, preferred_element_type=jnp.float32)
        iterate = (
            ns_first * iterate.astype(jnp.float32)
            + ns_second * cross.astype(jnp.float32)
            + ns_third * square
        ).astype(jnp.bfloat16)
    updated = (weights.astype(jnp.float32) + update_rate * iterate.astype(jnp.float32)).astype(
        jnp.bfloat16
    )
    applied = fast_apply(queries, updated)
    mixed = (attended + fw_scale * rms_norm(applied)).astype(jnp.bfloat16)
    projected = jnp.dot(
        lax.all_gather(mixed, "head", axis=1, tiled=True),
        out_weight,
        preferred_element_type=jnp.float32,
    )
    return projected.astype(jnp.bfloat16)


def solution(mesh):
    placed = (
        P("tok", "head"),
        P("tok", "head"),
        P("tok", "head"),
        P("tok", "head"),
        P("head", None, None, None),
        P(None, "head"),
    )

    def chosen(queries, *others):
        whole_window = queries.shape[0] * mesh.shape["tok"] <= WIN
        square = mesh.shape["head"] == PAIR * PAIR and mesh.shape["tok"] % PAIR == 0
        return (fused_body if whole_window and square else body)(queries, *others)

    return jax.shard_map(
        chosen, mesh=mesh, in_specs=placed, out_specs=P("tok", "head"), check_vma=False
    )
```
